32 devices in a mesh: band: 4 (over y, x), fft: 8 (over z, core).
Axes of the slice: x: 2, y: 2, z: 4, core: 2. Of those that a mesh axis runs over, the one named last changes fastest.
Arguments:
- wavefuncs: bfloat16 [2, 512, 16384], P(None, 'band', 'fft'), may hold values from -6 to 6
- ritz_coefs: bfloat16 [2, 512, 8], replicated, may hold values from -0.1875 to 0.1875
- potential: float32 [192, 192, 192], P(None, 'fft'), may hold values from -48 to 48
- projectors: bfloat16 [2, 8, 192, 192, 192], P(None, None, None, 'fft'), may hold values from -6 to 6
- kb_energies: float32 [512, 8], replicated, may hold values from 0.005 to 0.05
- sphere_map: int32 [16384], P('fft'), may hold values from 0 to 884735, as said below
- tile_atoms: int32 [12, 96, 24, 2], P(None, 'fft'), may hold values from 0 to 511
Outputs:
- rotated: bfloat16 [2, 8, 16384], P(None, 'band', 'fft')
- residual: bfloat16 [2, 8, 16384], P(None, 'band', 'fft')
- ritz_values: float32 [8], P('band')
The draws below stay inside these ranges and needn't reach their ends.
Inputs may be any that keep to these rules, and one draw needn't show every extreme that they name: `sphere_map`: within each run of 2048 coefficients no value appears twice.
All inputs are finite; a program needn't handle non-finite values.
Results may differ from the reference program's by a relative error of at most 0.014.
Values may be sent and summed in bfloat16 or wider, within the bound.
A program may use at most 576 MiB of HBM per device.

```python
import math
import jax
import jax.numpy as jnp
from jax import lax

NG = 192
NB = 512
BLK = 8
NATOM = 512
NPA = 8
AT = 2
TX = 16
TY = 2
TZ = 8
SLAB = 24
PW_SLAB = 2048
NPW = 16384


def draw_sphere_map(key, part):
    cell_count = SLAB * NG * NG
    slab_count = NPW // PW_SLAB

    def one_slab(position):
        inner = jax.random.permutation(jax.random.fold_in(key, position), cell_count - 2)[:PW_SLAB - 2].astype(jnp.int32) + 1
        whole = jnp.concatenate([jnp.zeros((1,), jnp.int32), jnp.full((1,), cell_count - 1, jnp.int32), inner])
        return jax.random.permutation(jax.random.fold_in(key, position + slab_count), whole)
    return jax.vmap(one_slab)(jnp.arange(slab_count, dtype=jnp.int32)).reshape(NPW).astype(jnp.int32)


def set_ends(array, rng, least, largest):
    place = [jax.random.randint(jax.random.fold_in(rng, axis), (), 0, length) for axis, length in enumerate(array.shape)]
    widest = array.shape.index(max(array.shape))
    beside = place[:widest] + [(place[widest] + 1) % array.shape[widest]] + place[widest + 1:]
    return array.at[tuple(place)].set(least).at[tuple(beside)].set(largest)


def block_levels(rng, shape, split, low, largest):
    loudness, own = 1.0, jax.random.fold_in(rng, 6)
    for dim, parts in split:
        steps = jnp.exp(jax.random.uniform(jax.random.fold_in(own, dim), (parts,), jnp.float32, low / len(split), largest / len(split)))
        loudness = loudness * jnp.repeat(steps, shape[dim] // parts).reshape([-1 if axis == dim else 1 for axis in range(len(shape))])
    return loudness


def noise(stream_key, dims, scale, reach, shards=(), kind=jnp.bfloat16):
    gain = block_levels(stream_key, dims, shards, -0.22, 0.18) if shards else 1.0
    drawn = jax.random.normal(stream_key, dims, jnp.float32) * scale * gain
    return jnp.minimum(jnp.maximum(drawn, -reach), reach).astype(kind)


def setup_inputs(seed: int = 0) -> dict:
    key_list = jax.random.split(jax.random.key(seed), 8)
    return {
        "wavefuncs": noise(key_list[0], (2, NB, NPW), 1.0, 6.0, ((1, 4), (2, 8))),
        "ritz_coefs": noise(key_list[1], (2, NB, BLK), (2 * NB) ** -0.5, 0.1875),
        "potential": noise(key_list[2], (NG, NG, NG), 8.0, 48.0, ((1, 8),), jnp.float32),
        "projectors": noise(key_list[3], (AT, NPA, NG, NG, NG), 1.0, 6.0, ((3, 8),)),
        "kb_energies": jnp.clip(jnp.exp(jax.random.uniform(key_list[4], (NATOM, NPA), jnp.float32, math.log(0.005), math.log(0.05))), 0.005, 0.05),
        "sphere_map": draw_sphere_map(jax.random.fold_in(key_list[7], 71), 0),
        "tile_atoms": set_ends(jax.random.randint(key_list[6], (NG // TX, NG // TY, NG // TZ, AT), 0, NATOM), jax.random.fold_in(key_list[6], 1), 0, NATOM - 1).astype(jnp.int32),
    }


def fourier_table(length, orient):
    indices = jnp.arange(length, dtype=jnp.int32)
    product_mod = indices[:, None] * indices[None, :] % length
    angles = product_mod.astype(jnp.float32) * (2.0 * math.pi / length)
    factor = 1.0 / math.sqrt(length)
    cosine = jnp.cos(angles) * factor
    sines = jnp.sin(angles) * (factor * orient)
    upper_rows = jnp.stack([cosine, -sines])
    lower_rows = jnp.stack([sines, cosine])
    return jnp.stack([upper_rows, lower_rows]).astype(jnp.bfloat16)

def realify(coefficient):
    return jnp.stack([jnp.stack([coefficient[0], -coefficient[1]]), jnp.stack([coefficient[1], coefficient[0]])])

def transform(values, table, dimension):
    source = 'cxyz'
    target = 'dxyz'
    source = source[:dimension] + 'n' + source[dimension + 1:]
    target = target[:dimension] + 'm' + target[dimension + 1:]
    return jnp.einsum('dcnm,' + source + '->' + target, table.astype(jnp.float32), values.astype(jnp.float32), precision=lax.Precision.HIGHEST)

def signed_square(position, length):
    signed = jnp.where(position < length // 2, position, position - length).astype(jnp.float32)
    return signed * signed

def reference(wavefuncs, ritz_coefs, potential, projectors, kb_energies, sphere_map, tile_atoms):
    rotated = jnp.einsum('dckj,ckg->djg', realify(ritz_coefs).astype(jnp.float32), wavefuncs.astype(jnp.float32), precision=lax.Precision.HIGHEST).astype(jnp.bfloat16)
    plane_count = NG * NG
    cell_index = jnp.arange(NPW, dtype=jnp.int32) // PW_SLAB * (SLAB * plane_count) + sphere_map.astype(jnp.int32)
    kinetic = 2.0 * (signed_square(cell_index // plane_count, NG) + signed_square(cell_index // NG % NG, NG) + signed_square(cell_index % NG, NG)) / float(NG * NG)
    proj_tiles = projectors.astype(jnp.float32).reshape(AT, NPA, NG // TX, TX, NG // TY, TY, NG // TZ, TZ)
    atom_list = tile_atoms.reshape(-1).astype(jnp.int32)
    inverse = fourier_table(NG, 1.0)
    forward = fourier_table(NG, -1.0)

    def apply_band(column):
        grid_field = jnp.zeros((2, NG * NG * NG), jnp.bfloat16).at[:, cell_index].set(column).reshape(2, NG, NG, NG)
        grid_field = transform(grid_field, inverse, 3).astype(jnp.bfloat16)
        grid_field = transform(grid_field, inverse, 2).astype(jnp.bfloat16)
        real_field = transform(grid_field, inverse, 1).astype(jnp.bfloat16)
        field_float = real_field.astype(jnp.float32)
        field_tiles = field_float.reshape(2, NG // TX, TX, NG // TY, TY, NG // TZ, TZ)
        intersections = jnp.einsum('slaxbycz,qaxbycz->abcslq', proj_tiles, field_tiles, precision=lax.Precision.HIGHEST)
        intersections = intersections.reshape(-1, NPA * 2)
        atom_coeff = jax.ops.segment_sum(intersections, atom_list, num_segments=NATOM)
        scaled = (kb_energies[:, :, None] * atom_coeff.reshape(NATOM, NPA, 2)).astype(jnp.bfloat16)
        picked = scaled[atom_list].astype(jnp.float32).reshape(NG // TX, NG // TY, NG // TZ, AT, NPA, 2)
        nonlocal_part = jnp.einsum('slaxbycz,abcslq->qaxbycz', proj_tiles, picked, precision=lax.Precision.HIGHEST).reshape(2, NG, NG, NG)
        combined = (potential[None] * field_float + nonlocal_part).astype(jnp.bfloat16)
        spectrum = transform(combined, forward, 1).astype(jnp.bfloat16)
        spectrum = transform(spectrum, forward, 2).astype(jnp.bfloat16)
        spectrum = transform(spectrum, forward, 3)
        return spectrum.reshape(2, -1)[:, cell_index]
    gathered = lax.map(apply_band, jnp.transpose(rotated, (1, 0, 2)))
    spectrum = jnp.transpose(gathered, (1, 0, 2))
    rotated_float = rotated.astype(jnp.float32)
    applied = kinetic[None, None, :] * rotated_float + spectrum
    numerator = lax.optimization_barrier(jnp.sum(rotated_float * applied, axis=(0, 2)))
    denominator = lax.optimization_barrier(jnp.sum(rotated_float * rotated_float, axis=(0, 2)))
    ritz_values = numerator / (denominator + 1e-06)
    residual = (applied - ritz_values[None, :, None] * rotated_float).astype(jnp.bfloat16)
    return (rotated, residual, ritz_values)
```

```python
import math

import jax
import jax.numpy as jnp
from jax import lax
from jax.experimental import pallas as pl
from jax.experimental.pallas import tpu as pltpu
from jax.sharding import PartitionSpec as P


def fourier_table(length, orient):
    indices = jnp.arange(length, dtype=jnp.int32)
    product_mod = indices[:, None] * indices[None, :] % length
    angles = product_mod.astype(jnp.float32) * (2.0 * math.pi / length)
    factor = 1.0 / math.sqrt(length)
    cosine = jnp.cos(angles) * factor
    sines = jnp.sin(angles) * (factor * orient)
    upper_rows = jnp.stack([cosine, -sines])
    lower_rows = jnp.stack([sines, cosine])
    return jnp.stack([upper_rows, lower_rows]).astype(jnp.bfloat16)


def realify(coefficient):
    return jnp.stack(
        [jnp.stack([coefficient[0], -coefficient[1]]), jnp.stack([coefficient[1], coefficient[0]])]
    )


def signed_square(position, length):
    signed = jnp.where(position < length // 2, position, position - length).astype(jnp.float32)
    return signed * signed


def largest_chunk(total, wanted):
    return wanted if total % wanted == 0 else total


def lane_chunks(width):
    return [(start, min(128, width - start)) for start in range(0, width, 128)]


def plane_waves(index_ref, tables, real_ref, imag_ref):
    yr_ref, yi_ref, zr_ref, zi_ref = tables
    rows = index_ref[0, 1:2, :]
    columns = index_ref[0, 2:3, :]
    length = yr_ref.shape[1]
    positions = lax.broadcasted_iota(jnp.int32, (length, rows.shape[1]), 0)
    row_pick = (positions == rows).astype(jnp.float32).astype(jnp.bfloat16)
    column_pick = (positions == columns).astype(jnp.float32).astype(jnp.bfloat16)
    yr = jnp.dot(yr_ref[...], row_pick, preferred_element_type=jnp.float32)
    yi = jnp.dot(yi_ref[...], row_pick, preferred_element_type=jnp.float32)
    zr = jnp.dot(zr_ref[...], column_pick, preferred_element_type=jnp.float32)
    zi = jnp.dot(zi_ref[...], column_pick, preferred_element_type=jnp.float32)
    depth = zr.shape[0]
    for y in range(yr.shape[0]):
        a, b = yr[y : y + 1], yi[y : y + 1]
        real_ref[y * depth : (y + 1) * depth, :] = (a * zr - b * zi).astype(jnp.bfloat16)
        imag_ref[y * depth : (y + 1) * depth, :] = (a * zi + b * zr).astype(jnp.bfloat16)


def spread_kernel(
    index_ref, coef_ref, turned_ref, yr, yi, zr, zi, out_ref, real_ref, imag_ref, a_ref, b_ref, sum_ref
):
    plane_waves(index_ref, (yr, yi, zr, zi), real_ref, imag_ref)
    planes = index_ref[0, 0:1, :]
    coefs = coef_ref[0]
    turned = turned_ref[0]
    count = coefs.shape[0]
    for x in range(a_ref.shape[0] // count):
        mask = (planes == x).astype(jnp.float32).astype(jnp.bfloat16)
        a_ref[x * count : (x + 1) * count, :] = coefs * mask
        b_ref[x * count : (x + 1) * count, :] = turned * mask
    dims = (((1,), (1,)), ((), ()))
    part = lax.dot_general(
        a_ref[...], real_ref[...], dims, preferred_element_type=jnp.float32
    ) + lax.dot_general(b_ref[...], imag_ref[...], dims, preferred_element_type=jnp.float32)

    @pl.when(pl.program_id(1) == 0)
    def _():
        sum_ref[...] = part

    @pl.when(pl.program_id(1) > 0)
    def _():
        sum_ref[...] += part

    @pl.when(pl.program_id(1) == pl.num_programs(1) - 1)
    def _():
        out_ref[0] = sum_ref[...].astype(jnp.bfloat16)


def sample_kernel(index_ref, field_ref, yr, yi, zr, zi, out_ref, real_ref, imag_ref):
    plane_waves(index_ref, (yr, yi, zr, zi), real_ref, imag_ref)
    planes = index_ref[0, 0:1, :]
    count = out_ref.shape[1]
    half = count // 2
    first = jnp.dot(field_ref[0], real_ref[...], preferred_element_type=jnp.float32)
    second = jnp.dot(field_ref[0], imag_ref[...], preferred_element_type=jnp.float32)
    total_first = jnp.zeros((count, planes.shape[1]), jnp.float32)
    total_second = jnp.zeros((count, planes.shape[1]), jnp.float32)
    for x in range(field_ref.shape[1] // count):
        mask = planes == x
        total_first += jnp.where(mask, first[x * count : (x + 1) * count], 0.0)
        total_second += jnp.where(mask, second[x * count : (x + 1) * count], 0.0)
    out_ref[0, :half] = total_first[:half] + total_second[half:]
    out_ref[0, half:] = total_first[half:] - total_second[:half]


def intersect_kernel(proj_ref, field_ref, tile_ref, out_ref, part_ref):
    count = field_ref.shape[1]
    slots = proj_ref.shape[1]
    for start, width in lane_chunks(proj_ref.shape[2]):

        def body(x, acc, start=start, width=width):
            proj = proj_ref[x, :, start : start + width].astype(jnp.float32)
            field = field_ref[x, :, start : start + width].astype(jnp.float32)
            return tuple(acc[k] + proj * field[k : k + 1] for k in range(count))

        zero = jnp.zeros((slots, width), jnp.float32)
        acc = lax.fori_loop(0, proj_ref.shape[0], body, (zero,) * count)
        for k in range(count):
            part_ref[k * slots : (k + 1) * slots, start : start + width] = acc[k]
    left = part_ref[...]
    total = None
    for _ in range(3):
        piece = left.astype(jnp.bfloat16)
        term = jnp.dot(piece, tile_ref[...], preferred_element_type=jnp.float32)
        total = term if total is None else total + term
        left = left - piece.astype(jnp.float32)
    out_ref[0] = total


def combine_kernel(proj_ref, field_ref, pot_ref, picked_ref, tile_ref, out_ref, weight_ref):
    count = field_ref.shape[1]
    slots = proj_ref.shape[1]
    weight_ref[...] = jnp.dot(
        picked_ref[0], tile_ref[...], preferred_element_type=jnp.float32
    )
    for start, width in lane_chunks(proj_ref.shape[2]):
        weights = [
            weight_ref[k * count : (k + 1) * count, start : start + width] for k in range(slots)
        ]

        def body(x, carry, start=start, width=width, weights=weights):
            proj = proj_ref[x, :, start : start + width].astype(jnp.float32)
            field = field_ref[x, :, start : start + width].astype(jnp.float32)
            total = pot_ref[x, :, start : start + width] * field
            for k in range(slots):
                total = total + weights[k] * proj[k : k + 1]
            out_ref[x, :, start : start + width] = total.astype(jnp.bfloat16)
            return carry

        lax.fori_loop(0, proj_ref.shape[0], body, 0)


def whole_spec(array):
    return pl.BlockSpec(array.shape, lambda *_: (0,) * array.ndim)


def spread_points(index, coefs, turned, tables, planes):
    slabs, count, points = coefs.shape
    cells = tables[0].shape[0] * tables[2].shape[0]
    chunk = largest_chunk(points, 512)
    rows = planes * count
    return pl.pallas_call(
        spread_kernel,
        out_shape=jax.ShapeDtypeStruct((slabs, rows, cells), jnp.bfloat16),
        grid=(slabs, points // chunk),
        in_specs=[
            pl.BlockSpec((1, 3, chunk), lambda s, k: (s, 0, k)),
            pl.BlockSpec((1, count, chunk), lambda s, k: (s, 0, k)),
            pl.BlockSpec((1, count, chunk), lambda s, k: (s, 0, k)),
        ]
        + [whole_spec(table) for table in tables],
        out_specs=pl.BlockSpec((1, rows, cells), lambda s, k: (s, 0, 0)),
        scratch_shapes=[
            pltpu.VMEM((cells, chunk), jnp.bfloat16),
            pltpu.VMEM((cells, chunk), jnp.bfloat16),
            pltpu.VMEM((rows, chunk), jnp.bfloat16),
            pltpu.VMEM((rows, chunk), jnp.bfloat16),
            pltpu.VMEM((rows, cells), jnp.float32),
        ],
        name="spread_points",
    )(index, coefs, turned, *tables)


def sample_points(index, field, tables, count):
    slabs, _, points = index.shape
    cells = field.shape[2]
    chunk = largest_chunk(points, 512)
    return pl.pallas_call(
        sample_kernel,
        out_shape=jax.ShapeDtypeStruct((slabs, count, points), jnp.float32),
        grid=(slabs, points // chunk),
        in_specs=[
            pl.BlockSpec((1, 3, chunk), lambda s, k: (s, 0, k)),
            pl.BlockSpec((1,) + field.shape[1:], lambda s, k: (s, 0, 0)),
        ]
        + [whole_spec(table) for table in tables],
        out_specs=pl.BlockSpec((1, count, chunk), lambda s, k: (s, 0, k)),
        scratch_shapes=[
            pltpu.VMEM((cells, chunk), jnp.bfloat16),
            pltpu.VMEM((cells, chunk), jnp.bfloat16),
        ],
        name="sample_points",
    )(index, field, *tables)


def intersect(proj, field, tiles, tile_depth):
    depth, slots, cells = proj.shape
    count = field.shape[1]
    blocks = depth // tile_depth
    return pl.pallas_call(
        intersect_kernel,
        out_shape=jax.ShapeDtypeStruct((blocks, count * slots, tiles.shape[1]), jnp.float32),
        grid=(blocks,),
        in_specs=[
            pl.BlockSpec((tile_depth, slots, cells), lambda a: (a, 0, 0)),
            pl.BlockSpec((tile_depth, count, cells), lambda a: (a, 0, 0)),
            whole_spec(tiles),
        ],
        out_specs=pl.BlockSpec((1, count * slots, tiles.shape[1]), lambda a: (a, 0, 0)),
        scratch_shapes=[pltpu.VMEM((count * slots, cells), jnp.float32)],
        name="intersect",
    )(proj, field, tiles)


def combine(proj, field, potential, picked, tiles, tile_depth):
    depth, slots, cells = proj.shape
    count = field.shape[1]
    blocks = depth // tile_depth
    return pl.pallas_call(
        combine_kernel,
        out_shape=jax.ShapeDtypeStruct(field.shape, jnp.bfloat16),
        grid=(blocks,),
        in_specs=[
            pl.BlockSpec((tile_depth, slots, cells), lambda a: (a, 0, 0)),
            pl.BlockSpec((tile_depth, count, cells), lambda a: (a, 0, 0)),
            pl.BlockSpec((tile_depth, 1, cells), lambda a: (a, 0, 0)),
            pl.BlockSpec((1,) + picked.shape[1:], lambda a: (a, 0, 0)),
            whole_spec(tiles),
        ],
        out_specs=pl.BlockSpec((tile_depth, count, cells), lambda a: (a, 0, 0)),
        scratch_shapes=[pltpu.VMEM((count * slots, cells), jnp.float32)],
        name="combine",
    )(proj, field, potential, picked, tiles)


def sum_to_owners(values, axis_name):
    return jnp.sum(
        lax.all_to_all(values, axis_name, split_axis=0, concat_axis=0, tiled=True), axis=0
    )


def shards(wavefuncs, ritz_coefs, potential, projectors, kb_energies, sphere_map, tile_atoms):
    band_count = lax.axis_size("band")
    fft_count = lax.axis_size("fft")
    band_index = lax.axis_index("band")
    fft_index = lax.axis_index("fft")
    slab_coefs = wavefuncs.shape[2]
    block = ritz_coefs.shape[2]
    per_device = block // band_count
    grid_size = potential.shape[0]
    slab_planes = potential.shape[1]
    atom_count, proj_count = kb_energies.shape
    slot_count = projectors.shape[0]
    slab_depth = grid_size // band_count
    z_offset = band_index * slab_depth
    z_tiles = tile_atoms.shape[2] // band_count
    x_tiles, y_tiles = tile_atoms.shape[:2]
    cells = slab_planes * slab_depth

    maps = lax.all_gather(sphere_map.reshape(1, slab_coefs), "fft", axis=0)
    index = jnp.concatenate(
        [maps // (grid_size * grid_size), maps // grid_size % grid_size, maps % grid_size], axis=1
    )
    owned = wavefuncs.shape[1]
    my_rows = lax.dynamic_slice_in_dim(ritz_coefs, band_index * owned, owned, 1)
    partial = jnp.einsum(
        "dckj,ckg->jdg", realify(my_rows), wavefuncs, preferred_element_type=jnp.float32
    )
    rotated_sum = sum_to_owners(
        partial.reshape(band_count, per_device, 2, slab_coefs), "band"
    )
    rotated = rotated_sum.astype(jnp.bfloat16).transpose(1, 0, 2)
    gathered = lax.all_gather(rotated, ("band", "fft"), axis=0)
    coefs = (
        gathered.reshape(band_count, fft_count, 2, per_device, slab_coefs)
        .transpose(1, 2, 0, 3, 4)
        .reshape(fft_count, 2 * block, slab_coefs)
    )
    turned = jnp.concatenate([-coefs[:, block:], coefs[:, :block]], axis=1)

    inverse = fourier_table(grid_size, 1.0)
    forward = fourier_table(grid_size, -1.0)
    parts = inverse[:, 0]
    y_rows = lax.dynamic_slice_in_dim(parts, fft_index * slab_planes, slab_planes, 2)
    z_rows = lax.dynamic_slice_in_dim(parts, z_offset, slab_depth, 2)
    tables = tuple(rows[part].T for rows in (y_rows, z_rows) for part in (0, 1))

    proj = lax.dynamic_slice_in_dim(projectors, z_offset, slab_depth, 4)
    proj = proj.reshape(slot_count * proj_count, grid_size, cells).transpose(1, 0, 2)
    local_potential = lax.dynamic_slice_in_dim(potential, z_offset, slab_depth, 2).reshape(
        grid_size, 1, cells
    )
    atom_ids = lax.dynamic_slice_in_dim(tile_atoms, band_index * z_tiles, z_tiles, 2)
    cell_ids = jnp.arange(cells, dtype=jnp.int32)
    tile_ids = (cell_ids // slab_depth) // (slab_planes // y_tiles) * z_tiles + (
        cell_ids % slab_depth
    ) // (slab_depth // z_tiles)
    tiles = (
        tile_ids[:, None] == jnp.arange(y_tiles * z_tiles, dtype=jnp.int32)[None, :]
    ).astype(jnp.bfloat16)
    owner_table = (
        atom_ids.reshape(-1, 1) == jnp.arange(atom_count, dtype=jnp.int32)[None, :]
    ).astype(jnp.bfloat16)

    spread = spread_points(index, coefs, turned, tables, slab_planes)
    spread = spread.reshape(grid_size, 2, block, cells)
    real_field = jnp.einsum(
        "dcnm,ncjr->mdjr", inverse, spread, preferred_element_type=jnp.float32
    ).astype(jnp.bfloat16)
    real_field = real_field.reshape(grid_size, 2 * block, cells)

    tile_depth = grid_size // x_tiles
    sums = intersect(proj, real_field, tiles, tile_depth)
    slot_sums = sums.reshape(
        x_tiles, 2 * block, slot_count, proj_count, y_tiles * z_tiles
    ).transpose(0, 4, 2, 3, 1)
    atom_sums = jnp.einsum(
        "ta,tk->ak",
        owner_table.astype(jnp.float32),
        slot_sums.reshape(atom_ids.size, proj_count * 2 * block),
        precision=lax.Precision.HIGHEST,
    )
    share = atom_count // band_count
    atom_sums = sum_to_owners(atom_sums.reshape(band_count, share, -1), "band")
    atom_sums = sum_to_owners(atom_sums.reshape(fft_count, share // fft_count, -1), "fft")
    my_atoms = share // fft_count
    my_energies = lax.dynamic_slice_in_dim(
        kb_energies, (band_index * fft_count + fft_index) * my_atoms, my_atoms, 0
    )
    scaled = (
        my_energies[:, :, None] * atom_sums.reshape(my_atoms, proj_count, 2 * block)
    ).astype(jnp.bfloat16)
    scaled = lax.all_gather(
        scaled.reshape(my_atoms, -1), ("band", "fft"), axis=0, tiled=True
    )
    picked = jnp.dot(owner_table, scaled, preferred_element_type=jnp.float32).astype(jnp.bfloat16)
    picked = (
        picked.reshape(x_tiles, y_tiles * z_tiles, slot_count * proj_count * 2 * block)
        .transpose(0, 2, 1)
    )
    combined = combine(proj, real_field, local_potential, picked, tiles.T, tile_depth)
    returned = jnp.einsum(
        "dcnm,ncjr->mdjr",
        forward,
        combined.reshape(grid_size, 2, block, cells),
        preferred_element_type=jnp.float32,
    ).astype(jnp.bfloat16)
    returned = returned.reshape(fft_count, slab_planes * 2 * block, cells)
    sampled = sample_points(index, returned, tables, 2 * block)
    sampled = sampled.reshape(fft_count, 2, band_count, per_device, slab_coefs).transpose(
        2, 0, 1, 3, 4
    )
    sampled = sum_to_owners(sum_to_owners(sampled, "band"), "fft")

    plane_ids = fft_index * slab_planes + sphere_map // (grid_size * grid_size)
    row_ids = sphere_map // grid_size % grid_size
    col_ids = sphere_map % grid_size
    kinetic = (
        2.0
        * (
            signed_square(plane_ids, grid_size)
            + signed_square(row_ids, grid_size)
            + signed_square(col_ids, grid_size)
        )
        / float(grid_size * grid_size)
    )
    rotated_float = rotated.astype(jnp.float32)
    applied = kinetic[None, None, :] * rotated_float + sampled
    numerator, denominator = lax.psum(
        (
            jnp.sum(rotated_float * applied, axis=(0, 2)),
            jnp.sum(rotated_float * rotated_float, axis=(0, 2)),
        ),
        "fft",
    )
    ritz_values = numerator / (denominator + 1e-06)
    residual = (applied - ritz_values[None, :, None] * rotated_float).astype(jnp.bfloat16)
    return (rotated, residual, ritz_values)


def solution(mesh):
    in_specs = (
        P(None, "band", "fft"),
        P(),
        P(None, "fft", None),
        P(None, None, None, "fft", None),
        P(),
        P("fft"),
        P(None, "fft", None, None),
    )
    out_specs = (P(None, "band", "fft"), P(None, "band", "fft"), P("band"))
    return jax.shard_map(shards, mesh=mesh, in_specs=in_specs, out_specs=out_specs, check_vma=False)
```

```python
import math

import jax
import jax.numpy as jnp
from jax import lax
from jax.experimental import pallas as pl
from jax.experimental.pallas import tpu as pltpu
from jax.sharding import PartitionSpec as P


def fourier_table(length, orient):
    indices = jnp.arange(length, dtype=jnp.int32)
    product_mod = indices[:, None] * indices[None, :] % length
    angles = product_mod.astype(jnp.float32) * (2.0 * math.pi / length)
    factor = 1.0 / math.sqrt(length)
    cosine = jnp.cos(angles) * factor
    sines = jnp.sin(angles) * (factor * orient)
    upper_rows = jnp.stack([cosine, -sines])
    lower_rows = jnp.stack([sines, cosine])
    return jnp.stack([upper_rows, lower_rows]).astype(jnp.bfloat16)


def realify(coefficient):
    return jnp.stack(
        [jnp.stack([coefficient[0], -coefficient[1]]), jnp.stack([coefficient[1], coefficient[0]])]
    )


def signed_square(position, length):
    signed = jnp.where(position < length // 2, position, position - length).astype(jnp.float32)
    return signed * signed


def largest_chunk(total, wanted):
    return wanted if total % wanted == 0 else total


def lane_chunks(width):
    return [(start, min(128, width - start)) for start in range(0, width, 128)]


def plane_waves(index_ref, tables, real_ref, imag_ref):
    yr_ref, yi_ref, zr_ref, zi_ref = tables
    rows = index_ref[0, 1:2, :]
    columns = index_ref[0, 2:3, :]
    length = yr_ref.shape[1]
    positions = lax.broadcasted_iota(jnp.int32, (length, rows.shape[1]), 0)
    row_pick = (positions == rows).astype(jnp.float32).astype(jnp.bfloat16)
    column_pick = (positions == columns).astype(jnp.float32).astype(jnp.bfloat16)
    yr = jnp.dot(yr_ref[...], row_pick, preferred_element_type=jnp.float32)
    yi = jnp.dot(yi_ref[...], row_pick, preferred_element_type=jnp.float32)
    zr = jnp.dot(zr_ref[...], column_pick, preferred_element_type=jnp.float32)
    zi = jnp.dot(zi_ref[...], column_pick, preferred_element_type=jnp.float32)
    depth = zr.shape[0]
    for y in range(yr.shape[0]):
        a, b = yr[y : y + 1], yi[y : y + 1]
        real_ref[y * depth : (y + 1) * depth, :] = (a * zr - b * zi).astype(jnp.bfloat16)
        imag_ref[y * depth : (y + 1) * depth, :] = (a * zi + b * zr).astype(jnp.bfloat16)


def spread_kernel(
    index_ref, coef_ref, turned_ref, yr, yi, zr, zi, out_ref, real_ref, imag_ref, a_ref, b_ref, sum_ref
):
    plane_waves(index_ref, (yr, yi, zr, zi), real_ref, imag_ref)
    planes = index_ref[0, 0:1, :]
    coefs = coef_ref[0]
    turned = turned_ref[0]
    count = coefs.shape[0]
    for x in range(a_ref.shape[0] // count):
        mask = (planes == x).astype(jnp.float32).astype(jnp.bfloat16)
        a_ref[x * count : (x + 1) * count, :] = coefs * mask
        b_ref[x * count : (x + 1) * count, :] = turned * mask
    dims = (((1,), (1,)), ((), ()))
    part = lax.dot_general(
        a_ref[...], real_ref[...], dims, preferred_element_type=jnp.float32
    ) + lax.dot_general(b_ref[...], imag_ref[...], dims, preferred_element_type=jnp.float32)

    @pl.when(pl.program_id(1) == 0)
    def _():
        sum_ref[...] = part

    @pl.when(pl.program_id(1) > 0)
    def _():
        sum_ref[...] += part

    @pl.when(pl.program_id(1) == pl.num_programs(1) - 1)
    def _():
        out_ref[0] = sum_ref[...].astype(jnp.bfloat16)


def sample_kernel(index_ref, field_ref, yr, yi, zr, zi, out_ref, real_ref, imag_ref):
    plane_waves(index_ref, (yr, yi, zr, zi), real_ref, imag_ref)
    planes = index_ref[0, 0:1, :]
    count = out_ref.shape[1]
    half = count // 2
    first = jnp.dot(field_ref[0], real_ref[...], preferred_element_type=jnp.float32)
    second = jnp.dot(field_ref[0], imag_ref[...], preferred_element_type=jnp.float32)
    total_first = jnp.zeros((count, planes.shape[1]), jnp.float32)
    total_second = jnp.zeros((count, planes.shape[1]), jnp.float32)
    for x in range(field_ref.shape[1] // count):
        mask = planes == x
        total_first += jnp.where(mask, first[x * count : (x + 1) * count], 0.0)
        total_second += jnp.where(mask, second[x * count : (x + 1) * count], 0.0)
    out_ref[0, :half] = total_first[:half] + total_second[half:]
    out_ref[0, half:] = total_first[half:] - total_second[:half]


def split_float(values):
    pieces = []
    for _ in range(3):
        pieces.append(values.astype(jnp.bfloat16))
        values = values - pieces[-1].astype(jnp.float32)
    return pieces


def intersect_kernel(proj_ref, field_ref, tile_ref, slot_ref, out_ref, part_ref):
    count = field_ref.shape[1]
    slots = proj_ref.shape[1]
    for start, width in lane_chunks(proj_ref.shape[2]):

        def body(x, acc, start=start, width=width):
            proj = proj_ref[x, :, start : start + width].astype(jnp.float32)
            field = field_ref[x, :, start : start + width].astype(jnp.float32)
            return tuple(acc[k] + proj * field[k : k + 1] for k in range(count))

        zero = jnp.zeros((slots, width), jnp.float32)
        acc = lax.fori_loop(0, proj_ref.shape[0], body, (zero,) * count)
        for k in range(count):
            part_ref[k * slots : (k + 1) * slots, start : start + width] = acc[k]
    total = sum(
        jnp.dot(piece, tile_ref[...], preferred_element_type=jnp.float32)
        for piece in split_float(part_ref[...])
    )
    pieces = split_float(total)
    slot_count, tile_count = slot_ref.shape[1:3]
    per_slot = slots // slot_count
    slot_of_row = lax.broadcasted_iota(jnp.int32, out_ref.shape, 0) // per_slot % slot_count
    atoms = lax.broadcasted_iota(jnp.int32, (tile_count, out_ref.shape[1]), 1)

    @pl.when(pl.program_id(0) == 0)
    def _():
        out_ref[...] = jnp.zeros_like(out_ref)

    for slot in range(slot_count):
        owner = (slot_ref[0, slot] == atoms).astype(jnp.float32).astype(jnp.bfloat16)
        owned = sum(jnp.dot(piece, owner, preferred_element_type=jnp.float32) for piece in pieces)
        out_ref[...] += jnp.where(slot_of_row == slot, owned, 0.0)


def combine_kernel(proj_ref, field_ref, pot_ref, picked_ref, tile_ref, out_ref, weight_ref):
    count = field_ref.shape[1]
    slots = proj_ref.shape[1]
    weight_ref[...] = jnp.dot(
        picked_ref[0], tile_ref[...], preferred_element_type=jnp.float32
    )
    for start, width in lane_chunks(proj_ref.shape[2]):
        weights = [
            weight_ref[k * count : (k + 1) * count, start : start + width] for k in range(slots)
        ]

        def body(x, carry, start=start, width=width, weights=weights):
            proj = proj_ref[x, :, start : start + width].astype(jnp.float32)
            field = field_ref[x, :, start : start + width].astype(jnp.float32)
            total = pot_ref[x, :, start : start + width] * field
            for k in range(slots):
                total = total + weights[k] * proj[k : k + 1]
            out_ref[x, :, start : start + width] = total.astype(jnp.bfloat16)
            return carry

        lax.fori_loop(0, proj_ref.shape[0], body, 0)


def whole_spec(array):
    return pl.BlockSpec(array.shape, lambda *_: (0,) * array.ndim)


def spread_points(index, coefs, turned, tables, planes):
    slabs, count, points = coefs.shape
    cells = tables[0].shape[0] * tables[2].shape[0]
    chunk = largest_chunk(points, 512)
    rows = planes * count
    return pl.pallas_call(
        spread_kernel,
        out_shape=jax.ShapeDtypeStruct((slabs, rows, cells), jnp.bfloat16),
        grid=(slabs, points // chunk),
        in_specs=[
            pl.BlockSpec((1, 3, chunk), lambda s, k: (s, 0, k)),
            pl.BlockSpec((1, count, chunk), lambda s, k: (s, 0, k)),
            pl.BlockSpec((1, count, chunk), lambda s, k: (s, 0, k)),
        ]
        + [whole_spec(table) for table in tables],
        out_specs=pl.BlockSpec((1, rows, cells), lambda s, k: (s, 0, 0)),
        scratch_shapes=[
            pltpu.VMEM((cells, chunk), jnp.bfloat16),
            pltpu.VMEM((cells, chunk), jnp.bfloat16),
            pltpu.VMEM((rows, chunk), jnp.bfloat16),
            pltpu.VMEM((rows, chunk), jnp.bfloat16),
            pltpu.VMEM((rows, cells), jnp.float32),
        ],
        name="spread_points",
    )(index, coefs, turned, *tables)


def sample_points(index, field, tables, count):
    slabs, _, points = index.shape
    cells = field.shape[2]
    chunk = largest_chunk(points, 512)
    return pl.pallas_call(
        sample_kernel,
        out_shape=jax.ShapeDtypeStruct((slabs, count, points), jnp.float32),
        grid=(slabs, points // chunk),
        in_specs=[
            pl.BlockSpec((1, 3, chunk), lambda s, k: (s, 0, k)),
            pl.BlockSpec((1,) + field.shape[1:], lambda s, k: (s, 0, 0)),
        ]
        + [whole_spec(table) for table in tables],
        out_specs=pl.BlockSpec((1, count, chunk), lambda s, k: (s, 0, k)),
        scratch_shapes=[
            pltpu.VMEM((cells, chunk), jnp.bfloat16),
            pltpu.VMEM((cells, chunk), jnp.bfloat16),
        ],
        name="sample_points",
    )(index, field, *tables)


def intersect(proj, field, tiles, slot_ids, tile_depth, atom_count):
    depth, slots, cells = proj.shape
    count = field.shape[1]
    blocks = depth // tile_depth
    return pl.pallas_call(
        intersect_kernel,
        out_shape=jax.ShapeDtypeStruct((count * slots, atom_count), jnp.float32),
        grid=(blocks,),
        in_specs=[
            pl.BlockSpec((tile_depth, slots, cells), lambda a: (a, 0, 0)),
            pl.BlockSpec((tile_depth, count, cells), lambda a: (a, 0, 0)),
            whole_spec(tiles),
            pl.BlockSpec((1,) + slot_ids.shape[1:], lambda a: (a, 0, 0, 0)),
        ],
        out_specs=pl.BlockSpec((count * slots, atom_count), lambda a: (0, 0)),
        scratch_shapes=[pltpu.VMEM((count * slots, cells), jnp.float32)],
        name="intersect",
    )(proj, field, tiles, slot_ids)


def combine(proj, field, potential, picked, tiles, tile_depth):
    depth, slots, cells = proj.shape
    count = field.shape[1]
    blocks = depth // tile_depth
    return pl.pallas_call(
        combine_kernel,
        out_shape=jax.ShapeDtypeStruct(field.shape, jnp.bfloat16),
        grid=(blocks,),
        in_specs=[
            pl.BlockSpec((tile_depth, slots, cells), lambda a: (a, 0, 0)),
            pl.BlockSpec((tile_depth, count, cells), lambda a: (a, 0, 0)),
            pl.BlockSpec((tile_depth, 1, cells), lambda a: (a, 0, 0)),
            pl.BlockSpec((1,) + picked.shape[1:], lambda a: (a, 0, 0)),
            whole_spec(tiles),
        ],
        out_specs=pl.BlockSpec((tile_depth, count, cells), lambda a: (a, 0, 0)),
        scratch_shapes=[pltpu.VMEM((count * slots, cells), jnp.float32)],
        name="combine",
    )(proj, field, potential, picked, tiles)


def sum_to_owners(values, axis_name):
    return jnp.sum(
        lax.all_to_all(values, axis_name, split_axis=0, concat_axis=0, tiled=True), axis=0
    )


def gather_blocks(values, axis_name):
    count = lax.axis_size(axis_name)
    copies = jnp.broadcast_to(values[None], (count,) + values.shape)
    return lax.all_to_all(copies, axis_name, split_axis=0, concat_axis=0, tiled=True)


def shards(wavefuncs, ritz_coefs, potential, projectors, kb_energies, sphere_map, tile_atoms):
    band_count = lax.axis_size("band")
    fft_count = lax.axis_size("fft")
    band_index = lax.axis_index("band")
    fft_index = lax.axis_index("fft")
    slab_coefs = wavefuncs.shape[2]
    block = ritz_coefs.shape[2]
    per_device = block // band_count
    grid_size = potential.shape[0]
    slab_planes = potential.shape[1]
    atom_count, proj_count = kb_energies.shape
    slot_count = projectors.shape[0]
    slab_depth = grid_size // band_count
    z_offset = band_index * slab_depth
    z_tiles = tile_atoms.shape[2] // band_count
    x_tiles, y_tiles = tile_atoms.shape[:2]
    cells = slab_planes * slab_depth

    maps = gather_blocks(sphere_map.reshape(1, slab_coefs), "fft")
    index = jnp.concatenate(
        [maps // (grid_size * grid_size), maps // grid_size % grid_size, maps % grid_size], axis=1
    )
    owned = wavefuncs.shape[1]
    my_rows = lax.dynamic_slice_in_dim(ritz_coefs, band_index * owned, owned, 1)
    partial = jnp.einsum(
        "dckj,ckg->jdg", realify(my_rows), wavefuncs, preferred_element_type=jnp.float32
    )
    rotated_sum = sum_to_owners(
        partial.reshape(band_count, per_device, 2, slab_coefs), "band"
    )
    rotated = rotated_sum.astype(jnp.bfloat16).transpose(1, 0, 2)
    gathered = gather_blocks(gather_blocks(rotated, "band"), "fft")
    coefs = gathered.transpose(0, 2, 1, 3, 4).reshape(fft_count, 2 * block, slab_coefs)
    turned = jnp.concatenate([-coefs[:, block:], coefs[:, :block]], axis=1)

    inverse = fourier_table(grid_size, 1.0)
    forward = fourier_table(grid_size, -1.0)
    parts = inverse[:, 0]
    y_rows = lax.dynamic_slice_in_dim(parts, fft_index * slab_planes, slab_planes, 2)
    z_rows = lax.dynamic_slice_in_dim(parts, z_offset, slab_depth, 2)
    tables = tuple(rows[part].T for rows in (y_rows, z_rows) for part in (0, 1))

    proj = lax.dynamic_slice_in_dim(projectors, z_offset, slab_depth, 4)
    proj = proj.reshape(slot_count * proj_count, grid_size, cells).transpose(1, 0, 2)
    local_potential = lax.dynamic_slice_in_dim(potential, z_offset, slab_depth, 2).reshape(
        grid_size, 1, cells
    )
    atom_ids = lax.dynamic_slice_in_dim(tile_atoms, band_index * z_tiles, z_tiles, 2)
    cell_ids = jnp.arange(cells, dtype=jnp.int32)
    tile_ids = (cell_ids // slab_depth) // (slab_planes // y_tiles) * z_tiles + (
        cell_ids % slab_depth
    ) // (slab_depth // z_tiles)
    tiles = (
        tile_ids[:, None] == jnp.arange(y_tiles * z_tiles, dtype=jnp.int32)[None, :]
    ).astype(jnp.bfloat16)
    owner_table = (
        atom_ids.reshape(-1, 1) == jnp.arange(atom_count, dtype=jnp.int32)[None, :]
    ).astype(jnp.bfloat16)

    spread = spread_points(index, coefs, turned, tables, slab_planes)
    spread = spread.reshape(grid_size, 2, block, cells)
    real_field = jnp.einsum(
        "dcnm,ncjr->mdjr", inverse, spread, preferred_element_type=jnp.float32
    ).astype(jnp.bfloat16)
    real_field = real_field.reshape(grid_size, 2 * block, cells)

    tile_depth = grid_size // x_tiles
    slot_ids = atom_ids.reshape(x_tiles, y_tiles * z_tiles, slot_count).transpose(0, 2, 1)
    sums = intersect(proj, real_field, tiles, slot_ids[..., None], tile_depth, atom_count)
    atom_sums = jnp.sum(
        sums.reshape(2 * block, slot_count, proj_count, atom_count), axis=1
    ).transpose(2, 1, 0)
    share = atom_count // band_count
    atom_sums = sum_to_owners(atom_sums.reshape(band_count, share, -1), "band")
    atom_sums = sum_to_owners(atom_sums.reshape(fft_count, share // fft_count, -1), "fft")
    my_atoms = share // fft_count
    my_energies = lax.dynamic_slice_in_dim(
        kb_energies, (band_index * fft_count + fft_index) * my_atoms, my_atoms, 0
    )
    scaled = (
        my_energies[:, :, None] * atom_sums.reshape(my_atoms, proj_count, 2 * block)
    ).astype(jnp.bfloat16)
    scaled = gather_blocks(gather_blocks(scaled.reshape(my_atoms, -1), "fft"), "band")
    scaled = scaled.reshape(atom_count, -1)
    picked = jnp.dot(owner_table, scaled, preferred_element_type=jnp.float32).astype(jnp.bfloat16)
    picked = (
        picked.reshape(x_tiles, y_tiles * z_tiles, slot_count * proj_count * 2 * block)
        .transpose(0, 2, 1)
    )
    combined = combine(proj, real_field, local_potential, picked, tiles.T, tile_depth)
    returned = jnp.einsum(
        "dcnm,ncjr->mdjr",
        forward,
        combined.reshape(grid_size, 2, block, cells),
        preferred_element_type=jnp.float32,
    ).astype(jnp.bfloat16)
    returned = returned.reshape(fft_count, slab_planes * 2 * block, cells)
    sampled = sample_points(index, returned, tables, 2 * block)
    sampled = sampled.reshape(fft_count, 2, band_count, per_device, slab_coefs).transpose(
        2, 0, 1, 3, 4
    )
    sampled = sum_to_owners(sum_to_owners(sampled, "band"), "fft")

    plane_ids = fft_index * slab_planes + sphere_map // (grid_size * grid_size)
    row_ids = sphere_map // grid_size % grid_size
    col_ids = sphere_map % grid_size
    kinetic = (
        2.0
        * (
            signed_square(plane_ids, grid_size)
            + signed_square(row_ids, grid_size)
            + signed_square(col_ids, grid_size)
        )
        / float(grid_size * grid_size)
    )
    rotated_float = rotated.astype(jnp.float32)
    applied = kinetic[None, None, :] * rotated_float + sampled
    products = jnp.stack(
        [
            jnp.sum(rotated_float * applied, axis=(0, 2)),
            jnp.sum(rotated_float * rotated_float, axis=(0, 2)),
        ]
    )
    numerator, denominator = jnp.sum(gather_blocks(products, "fft"), axis=0)
    ritz_values = numerator / (denominator + 1e-06)
    residual = (applied - ritz_values[None, :, None] * rotated_float).astype(jnp.bfloat16)
    return (rotated, residual, ritz_values)


def solution(mesh):
    in_specs = (
        P(None, "band", "fft"),
        P(),
        P(None, "fft", None),
        P(None, None, None, "fft", None),
        P(),
        P("fft"),
        P(None, "fft", None, None),
    )
    out_specs = (P(None, "band", "fft"), P(None, "band", "fft"), P("band"))
    return jax.shard_map(shards, mesh=mesh, in_specs=in_specs, out_specs=out_specs, check_vma=False)
```
